32 devices in a mesh: groups: 2 (over y), seq: 4 (over z), inner: 2 (over x), head: 2 (over core).
Axes of the slice: x: 2, y: 2, z: 4, core: 2. Of those that a mesh axis runs over, the one named last changes fastest.
Arguments:
- queries: bfloat16 [2048, 32, 128], P(('groups', 'seq', 'inner'), 'head'), parts along dimension 0, as said below
- keys: bfloat16 [2048, 4, 128], P(('groups', 'seq', 'inner'), 'head'), parts along dimension 0
- values: bfloat16 [2048, 4, 128], P(('groups', 'seq', 'inner'), 'head'), parts along dimension 0, may hold values from -6 to 6
- log_decay: float32 [2048, 4], P(('groups', 'seq', 'inner'), 'head'), parts along dimension 0, as said below
- gain: float32 [32, 128], P('head'), may hold values from 0.1 to 1.9
- block_list: int32 [32, 16], P(('groups', 'seq', 'inner')), parts along dimension 0, may hold values from 0 to 15, as said below
Outputs:
- attended: bfloat16 [2048, 32, 128], P(('groups', 'seq', 'inner'), 'head'), parts along dimension 0
The draws below stay inside these ranges and needn't reach their ends.
There are 2 independent parts, one for each index of `groups`. The reference program is written for one: setup_inputs(seed, part) draws one part's arguments, and reference() takes and returns one part's arrays. A program takes and returns all parts, laid end to end along the dimension named above; an argument that names none is the same for every part. Nothing has to cross between parts.
Inputs may be any that keep to these rules, and one draw needn't show every extreme that they name: Keys lie within -6 to 6; queries within -144 to 144. `log_decay`: each entry is below 0. `block_list`: entry 0 of row b is b. The sequence's pieces of 128 tokens fall into segments: piece p belongs to segment p modulo 2. Every entry of row b is a block at or before b in a piece of b's segment.
All inputs are finite; a program needn't handle non-finite values.
Results may differ from the reference program's by a relative error of at most 0.0017.
Values may be sent and summed in bfloat16 or wider, within the bound.
A program may use at most 64 MiB of HBM per device.

```python
import jax
import jax.numpy as jnp
from jax import lax

HEADS = 32
KEY_VALUE_HEADS = 4
DH = 128
BLK = 64
SEL = 16
TOK_DEV = 128
SEQUENCE_TOKENS = 1024
QBLOCKS = 16
N_INNER = 2


def key_field(key):
    base = jax.random.normal(jax.random.fold_in(key, 11), (SEQUENCE_TOKENS, KEY_VALUE_HEADS, DH), jnp.float32)
    return jnp.clip(base, -6.0, 6.0)


def draw_keys(key, part):
    return key_field(key).astype(jnp.bfloat16)


def draw_queries(key, part):
    base = jax.random.normal(jax.random.fold_in(key, 12), (SEQUENCE_TOKENS, HEADS, DH), jnp.float32)
    base = jnp.clip(base, -6.0, 6.0)
    return base.astype(jnp.bfloat16)


def draw_log_decay(key, part):
    order = jax.random.permutation(jax.random.fold_in(key, 21), KEY_VALUE_HEADS)
    fast = order < (KEY_VALUE_HEADS + 1) // 2
    fast_rate = jnp.exp(jax.random.uniform(jax.random.fold_in(key, 22), (KEY_VALUE_HEADS,), jnp.float32, jnp.log(1.0 / 50.0), jnp.log(1.0 / 30.0)))
    speed_ratio = jnp.where(fast, fast_rate, 0.5 / SEQUENCE_TOKENS)
    pieces = SEQUENCE_TOKENS // TOK_DEV
    multiplier_term = jnp.exp(jax.random.uniform(jax.random.fold_in(key, 23), (pieces, KEY_VALUE_HEADS), jnp.float32, jnp.log(0.5), jnp.log(2.0)))
    multiplier_term = jnp.repeat(multiplier_term, TOK_DEV, axis=0)
    random_wobble = jax.random.uniform(jax.random.fold_in(key, 24), (SEQUENCE_TOKENS, KEY_VALUE_HEADS), jnp.float32, 0.5, 1.5)
    marked_positions = jax.random.randint(jax.random.fold_in(key, 25), (3,), 0, SEQUENCE_TOKENS)
    dropped_amounts = jnp.log(jax.random.uniform(jax.random.fold_in(key, 26), (3, KEY_VALUE_HEADS), jnp.float32, 0.5, 0.8))
    sudden_spike = jnp.zeros((SEQUENCE_TOKENS, KEY_VALUE_HEADS), jnp.float32).at[marked_positions].add(dropped_amounts)
    return -speed_ratio[None, :] * multiplier_term * random_wobble + sudden_spike


def draw_block_list(key, part):
    per_piece = TOK_DEV // BLK
    number = jnp.arange(QBLOCKS)
    piece = number // per_piece
    within = number % per_piece
    outer = piece // N_INNER
    inner_idx = piece % N_INNER
    count = outer * per_piece + within + 1
    raw = jax.random.randint(jax.random.fold_in(key, 31), (QBLOCKS, SEL), 0, 2 ** 30)
    pick = raw % count[:, None]
    chosen = (pick // per_piece * N_INNER + inner_idx[:, None]) * per_piece + pick % per_piece
    chosen = chosen.at[:, 0].set(number)
    return chosen.astype(jnp.int32)


def level_of(stream_key, extent, cuts, least, top_value):
    factor_of = 1.0
    for axis_at, shards_of in cuts:
        draws = jax.random.uniform(jax.random.fold_in(jax.random.fold_in(stream_key, 6), axis_at), (shards_of,), jnp.float32, least / len(cuts), top_value / len(cuts))
        factor_of = factor_of * jnp.repeat(jnp.exp(draws), extent[axis_at] // shards_of).reshape((-1,) + (1,) * (len(extent) - 1 - axis_at))
    return factor_of


def gaussian(own_key, shape, deviation, reach, shards=(), dtype=jnp.bfloat16):
    array = jax.random.normal(own_key, shape, jnp.float32) * deviation
    if len(shards) > 0:
        array = level_of(own_key, shape, shards, -0.22, 0.18) * array
    return jnp.clip(array, min=-reach, max=reach).astype(dtype)


def setup_inputs(seed: int = 0, part: int = 0) -> dict:
    streams_of = jax.random.split(jax.random.key(seed), 7)
    part_splits = jax.random.split(jax.random.fold_in(streams_of[6], part), 7)
    queries = draw_queries(jax.random.fold_in(jax.random.fold_in(streams_of[6], part), 71), part)
    keys = draw_keys(jax.random.fold_in(jax.random.fold_in(streams_of[6], part), 71), part)
    values = gaussian(part_splits[2], (SEQUENCE_TOKENS, KEY_VALUE_HEADS, DH), 1.0, 6.0, ((0, 8), (1, 2)))
    log_decay = draw_log_decay(jax.random.fold_in(jax.random.fold_in(streams_of[6], part), 71), part)
    gain = jnp.clip(1.0 + 0.18 * jax.random.normal(streams_of[4], (HEADS, DH), jnp.float32), 0.1, 1.9)
    block_list = draw_block_list(jax.random.fold_in(jax.random.fold_in(streams_of[6], part), 71), part)
    return dict(queries=queries, keys=keys, values=values, log_decay=log_decay, gain=gain, block_list=block_list)


HIGH = lax.Precision.HIGHEST

def linear_branch(queries, keys, values, log_decay):
    rep = HEADS // KEY_VALUE_HEADS
    count = SEQUENCE_TOKENS // TOK_DEV
    qall = queries.astype(jnp.float32).reshape(count, TOK_DEV, KEY_VALUE_HEADS, rep, DH)
    kall = keys.astype(jnp.float32).reshape(count, TOK_DEV, KEY_VALUE_HEADS, DH)
    vall = values.astype(jnp.float32).reshape(count, TOK_DEV, KEY_VALUE_HEADS, DH)
    dall = log_decay.reshape(count, TOK_DEV, KEY_VALUE_HEADS)
    causal = jnp.arange(TOK_DEV)[:, None] >= jnp.arange(TOK_DEV)[None, :]

    def step(state, piece):
        qf, kf, vf, dec = piece
        cum = jnp.cumsum(dec, axis=0)
        total = cum[-1]
        scores = jnp.einsum('tkrd,skd->krts', qf, kf, precision=HIGH)
        diff = cum.T[:, :, None] - cum.T[:, None, :]
        weight = jnp.where(causal[None], jnp.exp(jnp.minimum(diff, 0.0)), 0.0)
        intra = jnp.einsum('krts,skd->tkrd', scores * weight[:, None], vf, precision=HIGH)
        inter = jnp.exp(cum)[:, :, None, None] * jnp.einsum('tkrd,kde->tkre', qf, state, precision=HIGH)
        tail = jnp.exp(total[None, :] - cum)
        own_state = jnp.einsum('skd,ske->kde', kf * tail[:, :, None], vf, precision=HIGH)
        new_state = jnp.exp(total)[:, None, None] * state + own_state
        return (new_state, (intra + inter).reshape(TOK_DEV, HEADS, DH))
    start = jnp.zeros((KEY_VALUE_HEADS, DH, DH), jnp.float32)
    final_state, pieces = lax.scan(step, start, (qall, kall, vall, dall))
    return pieces.reshape(SEQUENCE_TOKENS, HEADS, DH)

def sparse_branch(queries, keys, values, block_list):
    rep = HEADS // KEY_VALUE_HEADS
    kblocks = keys.astype(jnp.float32).reshape(QBLOCKS, BLK, KEY_VALUE_HEADS, DH)
    vblocks = values.astype(jnp.float32).reshape(QBLOCKS, BLK, KEY_VALUE_HEADS, DH)
    qblocks = queries.astype(jnp.float32).reshape(QBLOCKS, BLK, KEY_VALUE_HEADS, rep, DH)
    lower = jnp.arange(SEL)[None, :] < jnp.arange(SEL)[:, None]

    def one_block(args):
        qblk, sel, number = args
        pk = kblocks[sel]
        pv = vblocks[sel]
        repeat = jnp.any((sel[:, None] == sel[None, :]) & lower, axis=1)
        keep = jnp.logical_not(repeat)
        qpos = number * BLK + jnp.arange(BLK)
        kpos = sel[:, None] * BLK + jnp.arange(BLK)[None, :]
        valid = keep[None, :, None] & (kpos[None] <= qpos[:, None, None])
        score = jnp.einsum('qkrd,jukd->krqju', qblk, pk, precision=HIGH) * DH ** (-0.5)
        score = jnp.where(valid[None, None], score, -1e+30)
        top = lax.optimization_barrier(jnp.max(score, axis=(3, 4), keepdims=True))
        expo = jnp.where(valid[None, None], jnp.exp(score - top), 0.0)
        denom = lax.optimization_barrier(jnp.sum(expo, axis=(3, 4)))
        weights = expo.astype(jnp.bfloat16).astype(jnp.float32)
        out = jnp.einsum('krqju,jukd->qkrd', weights, pv, precision=HIGH)
        return out / jnp.transpose(denom, (2, 0, 1))[:, :, :, None]
    numbers = jnp.arange(QBLOCKS).astype(jnp.int32)
    outs = lax.map(one_block, (qblocks, block_list, numbers))
    return outs.reshape(SEQUENCE_TOKENS, HEADS, DH)

def reference(queries, keys, values, log_decay, gain, block_list):
    linear = linear_branch(queries, keys, values, log_decay)
    normed = linear * lax.rsqrt(lax.optimization_barrier(jnp.mean(linear * linear, axis=-1, keepdims=True)) + 1e-06) * gain[None]
    sparse = sparse_branch(queries, keys, values, block_list)
    return (normed + sparse).astype(jnp.bfloat16)
```

```python
import functools

import jax
import jax.numpy as jnp
from jax import lax
from jax.experimental import pallas as pl
from jax.experimental.pallas import tpu as pltpu
from jax.sharding import PartitionSpec as P

BLK = 64
HIGH = lax.Precision.HIGHEST
MESH = pl.DeviceIdType.MESH
LD_ROWS = 8
F32 = jnp.float32
BF16 = jnp.bfloat16
LOG2E = 1.4426950408889634


def iota(shape, dim):
    return lax.broadcasted_iota(jnp.int32, shape, dim)


def dot(a, b, dims=((1,), (0,)), precision=None):
    return lax.dot_general(
        a, b, (dims, ((), ())), precision=precision, preferred_element_type=F32
    )


def halves(x):
    hi = x.astype(BF16)
    return hi, (x - hi.astype(F32)).astype(BF16)


def kernel(
    n_seq, n_inner, kv,
    q_hbm, k_hbm, v_hbm, ld_ref, gain_ref, list_ref,
    out_ref,
    qbuf, kbuf, vbuf, ldbuf, qs, kd, vd, bias, lin, sp, msg, got,
    local_sem, k_send, k_recv, v_send, v_recv, ld_send, ld_recv, m_send, m_recv,
):
    z = lax.axis_index("seq")
    x = lax.axis_index("inner")
    pieces = n_seq * n_inner
    tokens, heads, width = qbuf.shape
    rep = heads // kv
    rows = tokens * rep
    per_piece = tokens // BLK
    keys_all = n_seq * tokens

    q_copy = pltpu.make_async_copy(q_hbm, qbuf, local_sem.at[0])
    k_copy = pltpu.make_async_copy(k_hbm, kbuf.at[z], local_sem.at[1])
    v_copy = pltpu.make_async_copy(v_hbm, vbuf.at[z], local_sem.at[2])
    l_copy = pltpu.make_async_copy(ld_ref, ldbuf.at[z * n_inner], local_sem.at[3])
    for copy in (k_copy, v_copy, l_copy, q_copy):
        copy.start()

    me = z * n_inner + x
    barrier = pltpu.get_barrier_semaphore()

    @pl.loop(1, pieces)
    def _(o):
        p = lax.rem(me + o, pieces)
        pl.semaphore_signal(
            barrier, inc=1, device_id={"seq": p // n_inner, "inner": lax.rem(p, n_inner)},
            device_id_type=MESH)

    pl.semaphore_wait(barrier, pieces - 1)

    def kv_copies(o):
        to = {"seq": lax.rem(z + o, n_seq)}
        return (
            pltpu.make_async_remote_copy(
                src_ref=k_hbm, dst_ref=kbuf.at[z], send_sem=k_send.at[o],
                recv_sem=k_recv.at[o], device_id=to, device_id_type=MESH),
            pltpu.make_async_remote_copy(
                src_ref=v_hbm, dst_ref=vbuf.at[z], send_sem=v_send.at[o],
                recv_sem=v_recv.at[o], device_id=to, device_id_type=MESH),
        )

    def ld_copy(o):
        oz, ox = o // n_inner, lax.rem(o, n_inner)
        slot = z * n_inner + lax.rem(n_inner - ox, n_inner)
        return pltpu.make_async_remote_copy(
            src_ref=ld_ref, dst_ref=ldbuf.at[slot], send_sem=ld_send.at[o],
            recv_sem=ld_recv.at[o],
            device_id={"seq": lax.rem(z + oz, n_seq), "inner": lax.rem(x + ox, n_inner)},
            device_id_type=MESH)

    def ld_arrival(o):
        oz, ox = o // n_inner, lax.rem(o, n_inner)
        slot = lax.rem(z + n_seq - oz, n_seq) * n_inner + lax.rem(n_inner - ox, n_inner)
        return pltpu.make_async_remote_copy(
            src_ref=ld_ref, dst_ref=ldbuf.at[slot], send_sem=ld_send.at[o],
            recv_sem=ld_recv.at[o], device_id={"seq": z}, device_id_type=MESH)

    def kv_arrivals(o):
        slot = lax.rem(z + n_seq - o, n_seq)
        return (
            pltpu.make_async_remote_copy(
                src_ref=k_hbm, dst_ref=kbuf.at[slot], send_sem=k_send.at[o],
                recv_sem=k_recv.at[o], device_id={"seq": z}, device_id_type=MESH),
            pltpu.make_async_remote_copy(
                src_ref=v_hbm, dst_ref=vbuf.at[slot], send_sem=v_send.at[o],
                recv_sem=v_recv.at[o], device_id={"seq": z}, device_id_type=MESH),
        )

    @pl.loop(1, pieces)
    def _(o):
        ld_copy(o).start()

    for o in range(1, n_seq):
        for copy in kv_copies(o):
            copy.start()

    lanes = iota((kv * tokens, kv * tokens), 1)
    subs = iota((kv * tokens, kv * tokens), 0)
    by_head = jnp.where(
        lanes == lax.rem(subs, tokens) * kv + subs // tokens, 1.0, 0.0
    ).astype(BF16)

    ld = ld_ref[...]
    upto = jnp.where(iota((tokens, tokens), 0) <= iota((tokens, tokens), 1), 1.0, 0.0)
    cum_lane = dot(ld, upto, precision=HIGH)
    row_tok = iota((rows, tokens), 0) // rep
    lane_tok = iota((rows, tokens), 1)
    seen = row_tok >= lane_tok
    cum_row = dot(jnp.where(seen, 1.0, 0.0), ld, ((1,), (1,)), HIGH)

    k_copy.wait()
    v_copy.wait()
    k_own = dot(by_head, kbuf[z]).astype(BF16)
    v_own = dot(by_head, vbuf[z]).astype(BF16)
    q_copy.wait()
    qf = qbuf[...].astype(F32)
    for g in range(kv):
        q_g = qf[:, g * rep:(g + 1) * rep, :].reshape(rows, width).astype(BF16)
        qs[g] = q_g
        k_g = k_own[g * tokens:(g + 1) * tokens]
        v_g = v_own[g * tokens:(g + 1) * tokens]
        diff = cum_row[:, g:g + 1] - cum_lane[g:g + 1, :]
        weight = jnp.where(seen, jnp.exp(jnp.minimum(diff, 0.0)), 0.0)
        hi, lo = halves(dot(q_g, k_g, ((1,), (1,))) * weight)
        lin[g] = dot(
            jnp.concatenate([hi, lo], axis=1), jnp.concatenate([v_g, v_g], axis=0))

    key_lane = iota((1, keys_all), 1)
    key_block = (
        (key_lane // tokens * n_inner + x) * per_piece + lax.rem(key_lane, tokens) // BLK
    )
    key_pos = key_block * BLK + lax.rem(key_lane, BLK)
    listed = list_ref[...]
    for b in range(per_piece):
        member = key_block == listed[b:b + 1, 0:1]
        for i in range(1, listed.shape[1]):
            member = jnp.logical_or(member, key_block == listed[b:b + 1, i:i + 1])
        limit = jnp.where(member, key_pos, jnp.int32(2**30))
        query = me * tokens + b * BLK + iota((BLK * rep, 1), 0) // rep
        bias[b * BLK * rep:(b + 1) * BLK * rep, :] = jnp.where(limit <= query, 0.0, -1e30)

    l_copy.wait()

    @pl.loop(1, pieces)
    def _(o):
        ld_arrival(o).wait_recv()

    n_ld = pieces * LD_ROWS
    ld_all = ldbuf[...].reshape(n_ld, tokens)
    after = jnp.where(iota((tokens, tokens), 0) < iota((tokens, tokens), 1), 1.0, 0.0)
    tail = dot(after, ld_all, ((1,), (1,)), HIGH)
    total = dot(jnp.ones((8, tokens), F32), ld_all, ((1,), (1,)), HIGH)[0:1]

    def piece_of(r):
        i = r // LD_ROWS
        return i // n_inner * n_inner + lax.rem(x + lax.rem(i, n_inner), n_inner)

    r0, r1 = iota((n_ld, n_ld), 0), iota((n_ld, n_ld), 1)
    between = (
        (lax.rem(r0, LD_ROWS) == lax.rem(r1, LD_ROWS))
        & (piece_of(r0) > piece_of(r1)) & (piece_of(r0) < z * n_inner)
    )
    rest = dot(
        jnp.broadcast_to(total, (8, n_ld)), jnp.where(between, 1.0, 0.0), precision=HIGH
    )[0:1]
    r = iota((1, n_ld), 1)
    far = jnp.where(piece_of(r) < z * n_inner, jnp.exp(tail + rest), 0.0)

    def span(g, first, last):
        inside = (lax.rem(r, LD_ROWS) == g) & (piece_of(r) >= first) & (piece_of(r) < last)
        return jnp.exp(jnp.sum(jnp.where(inside, total, 0.0), axis=1, keepdims=True))

    own_tail = dot(after, ld, ((1,), (1,)), HIGH)

    def outer(k, weighted):
        hi, lo = halves(weighted)
        return dot(
            jnp.concatenate([k, k], axis=0), jnp.concatenate([hi, lo], axis=0), ((0,), (0,)))

    own = []
    for g in range(kv):
        k_g = k_own[g * tokens:(g + 1) * tokens]
        v_g = v_own[g * tokens:(g + 1) * tokens].astype(F32)
        own.append(outer(k_g, v_g * jnp.exp(own_tail[:, g:g + 1])))

    for o in range(1, n_seq):
        for copy in kv_arrivals(o):
            copy.wait_recv()
    state = [jnp.zeros((width, width), F32) for _ in range(kv)]
    for s in range(n_seq):
        k_s = dot(by_head, kbuf[s]).astype(BF16)
        v_s = dot(by_head, vbuf[s])
        for g in range(kv):
            k_g = k_s[g * tokens:(g + 1) * tokens]
            v_g = v_s[g * tokens:(g + 1) * tokens]
            kd[g, s * tokens:(s + 1) * tokens, :] = k_g
            vd[g, s * tokens:(s + 1) * tokens, :] = v_g.astype(BF16)
            col = s * n_inner * LD_ROWS + g
            state[g] = state[g] + outer(k_g, v_g * far[:, col:col + 1])

    start = z * n_inner
    for g in range(kv):
        msg[0, g] = state[g]
        msg[1, g] = state[g] * span(g, start, me + 1) + own[g]

    def m_copy(o):
        to = lax.rem(x + o, n_inner)
        return pltpu.make_async_remote_copy(
            src_ref=msg.at[jnp.where(to > x, 1, 0)], dst_ref=got.at[o],
            send_sem=m_send.at[o], recv_sem=m_recv.at[o],
            device_id={"inner": to}, device_id_type=MESH)

    for o in range(1, n_inner):
        m_copy(o).start()

    step = min(rows, 256)
    scale = width ** (-0.5) * LOG2E

    @pl.loop(0, rows // step)
    def _(c):
        at = pl.ds(pl.multiple_of(c * step, step), step)
        for g in range(kv):
            score = dot(qs[g, at, :], kd[g], ((1,), (1,))) + bias[at, :]
            top = jnp.max(score, axis=1, keepdims=True)
            expo = jnp.exp2((score - top) * scale)
            denom = jnp.sum(expo, axis=1, keepdims=True)
            sp[g, at, :] = dot(expo.astype(BF16), vd[g]) / denom

    prior = [state[g] * span(g, start, me) for g in range(kv)]
    for o in range(1, n_inner):
        m_copy(o).wait_recv()
        source = lax.rem(x + n_inner - o, n_inner)
        first = jnp.where(source < x, start + source + 1, start)
        for g in range(kv):
            prior[g] = prior[g] + got[o, g] * span(g, first, me)

    done = []
    for g in range(kv):
        hi, lo = halves(prior[g])
        q_g = qs[g]
        inter = dot(
            jnp.concatenate([q_g, q_g], axis=1), jnp.concatenate([hi, lo], axis=0))
        linear = lin[g] + inter * jnp.exp(cum_row[:, g:g + 1])
        norm = lax.rsqrt(jnp.mean(linear * linear, axis=1, keepdims=True) + 1e-6)
        scaled = (linear * norm).reshape(tokens, rep, width) * gain_ref[g * rep:(g + 1) * rep, :][None]
        done.append(scaled + sp[g].reshape(tokens, rep, width))
    out_ref[...] = jnp.concatenate(done, axis=1).astype(out_ref.dtype)

    @pl.loop(1, pieces)
    def _(o):
        ld_copy(o).wait_send()

    for o in range(1, n_seq):
        for copy in kv_copies(o):
            copy.wait_send()
    for o in range(1, n_inner):
        m_copy(o).wait_send()


def shards(n_seq, n_inner, queries, keys, values, log_decay, gain, block_list):
    tokens, heads, width = queries.shape
    kv = keys.shape[1]
    rows = tokens * (heads // kv)
    pieces = n_seq * n_inner
    decay = jnp.pad(log_decay.T, ((0, LD_ROWS - kv), (0, 0)))
    vmem = pl.BlockSpec(memory_space=pltpu.VMEM)
    anywhere = pl.BlockSpec(memory_space=pl.ANY)
    dma = pltpu.SemaphoreType.DMA
    return pl.pallas_call(
        functools.partial(kernel, n_seq, n_inner, kv),
        out_shape=jax.ShapeDtypeStruct(queries.shape, queries.dtype),
        in_specs=[anywhere, anywhere, anywhere, vmem, vmem, vmem],
        out_specs=vmem,
        scratch_shapes=[
            pltpu.VMEM(queries.shape, BF16),
            pltpu.VMEM((n_seq, kv * tokens, width), BF16),
            pltpu.VMEM((n_seq, kv * tokens, width), BF16),
            pltpu.VMEM((pieces, LD_ROWS, tokens), F32),
            pltpu.VMEM((kv, rows, width), BF16),
            pltpu.VMEM((kv, n_seq * tokens, width), BF16),
            pltpu.VMEM((kv, n_seq * tokens, width), BF16),
            pltpu.VMEM((rows, n_seq * tokens), F32),
            pltpu.VMEM((kv, rows, width), F32),
            pltpu.VMEM((kv, rows, width), F32),
            pltpu.VMEM((2, kv, width, width), F32),
            pltpu.VMEM((n_inner, kv, width, width), F32),
            dma((4,)),
            dma((n_seq,)), dma((n_seq,)), dma((n_seq,)), dma((n_seq,)),
            dma((pieces,)), dma((pieces,)),
            dma((n_inner,)), dma((n_inner,)),
        ],
        compiler_params=pltpu.CompilerParams(collective_id=0, has_side_effects=True),
        name="prefill",
    )(
        queries, keys.reshape(tokens * kv, width), values.reshape(tokens * kv, width),
        decay, gain, block_list,
    )


def solution(mesh):
    return jax.shard_map(
        functools.partial(shards, mesh.shape["seq"], mesh.shape["inner"]),
        mesh=mesh,
        in_specs=(
            P(("groups", "seq", "inner"), "head", None),
            P(("groups", "seq", "inner"), "head", None),
            P(("groups", "seq", "inner"), "head", None),
            P(("groups", "seq", "inner"), "head"),
            P("head", None),
            P(("groups", "seq", "inner"), None),
        ),
        out_specs=P(("groups", "seq", "inner"), "head", None),
        check_vma=False,
    )
```

```python
import functools

import jax
import jax.numpy as jnp
from jax import lax
from jax.experimental import pallas as pl
from jax.experimental.pallas import tpu as pltpu
from jax.sharding import PartitionSpec as P

BLK = 64
HIGH = lax.Precision.HIGHEST
MESH = pl.DeviceIdType.MESH
LD_ROWS = 8
F32 = jnp.float32
BF16 = jnp.bfloat16
LOG2E = 1.4426950408889634


def iota(shape, dim):
    return lax.broadcasted_iota(jnp.int32, shape, dim)


def dot(a, b, dims=((1,), (0,)), precision=None):
    return lax.dot_general(
        a, b, (dims, ((), ())), precision=precision, preferred_element_type=F32
    )


def halves(x):
    hi = x.astype(BF16)
    return hi, (x - hi.astype(F32)).astype(BF16)


def kernel(
    n_seq, n_inner, kv,
    q_hbm, k_hbm, v_hbm, ld_hbm, gain_ref, list_ref,
    out_ref,
    qbuf, kbuf, vbuf, ldbuf, qs, kd, vd, bias, lin, sp, msg, got,
    local_sem, k_send, k_recv, v_send, v_recv, l_send, l_recv, x_send, x_recv,
    m_send, m_recv,
):
    z = lax.axis_index("seq")
    x = lax.axis_index("inner")
    tokens, heads, width = qbuf.shape
    rep = heads // kv
    rows = tokens * rep
    per_piece = tokens // BLK
    keys_all = n_seq * tokens
    has_next, has_last = z < n_seq - 1, z > 0

    ldbuf[...] = jnp.zeros_like(ldbuf)
    q_copy = pltpu.make_async_copy(q_hbm, qbuf, local_sem.at[0])
    k_copy = pltpu.make_async_copy(k_hbm, kbuf.at[0], local_sem.at[1])
    v_copy = pltpu.make_async_copy(v_hbm, vbuf.at[0], local_sem.at[2])
    l_copy = pltpu.make_async_copy(ld_hbm, ldbuf.at[0, 0, 0:kv], local_sem.at[3])
    for copy in (l_copy, k_copy, v_copy, q_copy):
        copy.start()

    barrier = pltpu.get_barrier_semaphore()

    @pl.when(has_next)
    def _():
        pl.semaphore_signal(barrier, inc=1, device_id={"seq": z + 1}, device_id_type=MESH)

    @pl.when(has_last)
    def _():
        pl.semaphore_signal(barrier, inc=1, device_id={"seq": z - 1}, device_id_type=MESH)

    for o in range(1, n_inner):
        pl.semaphore_signal(
            barrier, inc=1, device_id={"inner": lax.rem(x + o, n_inner)}, device_id_type=MESH)
    ends = jnp.where(has_next, 1, 0) + jnp.where(has_last, 1, 0)
    pl.semaphore_wait(barrier, n_inner - 1 + ends)

    def hop(src, dst, send, recv):
        return pltpu.make_async_remote_copy(
            src_ref=src, dst_ref=dst, send_sem=send, recv_sem=recv,
            device_id={"seq": z + 1}, device_id_type=MESH)

    def k_hop(j):
        return hop(
            k_hbm if j == 0 else kbuf.at[j], kbuf.at[j + 1], k_send.at[j], k_recv.at[j + 1])

    def v_hop(j):
        return hop(
            v_hbm if j == 0 else vbuf.at[j], vbuf.at[j + 1], v_send.at[j], v_recv.at[j + 1])

    def l_hop(j):
        return hop(
            ldbuf.at[j, :, 0:kv], ldbuf.at[j + 1, :, 0:kv], l_send.at[j], l_recv.at[j + 1])

    def relay(hops, j):
        @pl.when(z >= j)
        def _():
            hops(j - 1).wait_recv()

        if j < n_seq - 1:

            @pl.when((z >= j) & has_next)
            def _():
                hops(j).start()

    def x_copy(o):
        return pltpu.make_async_remote_copy(
            src_ref=ld_hbm, dst_ref=ldbuf.at[0, n_inner - o, 0:kv], send_sem=x_send.at[o],
            recv_sem=x_recv.at[o], device_id={"inner": lax.rem(x + o, n_inner)},
            device_id_type=MESH)

    @pl.when(has_next)
    def _():
        k_hop(0).start()
        v_hop(0).start()

    for o in range(1, n_inner):
        x_copy(o).start()

    lanes = iota((kv * tokens, kv * tokens), 1)
    subs = iota((kv * tokens, kv * tokens), 0)
    by_head = jnp.where(
        lanes == lax.rem(subs, tokens) * kv + subs // tokens, 1.0, 0.0
    ).astype(BF16)

    l_copy.wait()
    ld = ldbuf[0, 0]
    upto = jnp.where(iota((tokens, tokens), 0) <= iota((tokens, tokens), 1), 1.0, 0.0)
    after = jnp.where(iota((tokens, tokens), 0) < iota((tokens, tokens), 1), 1.0, 0.0)
    cum_lane = dot(ld, upto, precision=HIGH)
    row_tok = iota((rows, tokens), 0) // rep
    lane_tok = iota((rows, tokens), 1)
    seen = row_tok >= lane_tok
    cum_row = dot(jnp.where(seen, 1.0, 0.0), ld, ((1,), (1,)), HIGH)
    own_tail = dot(after, ld, ((1,), (1,)), HIGH)

    def outer(k, weighted):
        hi, lo = halves(weighted)
        return dot(
            jnp.concatenate([k, k], axis=0), jnp.concatenate([hi, lo], axis=0), ((0,), (0,)))

    def split(j):
        k_j = dot(by_head, kbuf[j]).astype(BF16)
        v_j = dot(by_head, vbuf[j])
        out = []
        for g in range(kv):
            k_g = k_j[g * tokens:(g + 1) * tokens]
            v_g = v_j[g * tokens:(g + 1) * tokens]
            kd[g, j * tokens:(j + 1) * tokens, :] = k_g
            vd[g, j * tokens:(j + 1) * tokens, :] = v_g.astype(BF16)
            out.append((k_g, v_g))
        return out

    k_copy.wait()
    v_copy.wait()
    mine = split(0)
    own = [outer(k_g, v_g * jnp.exp(own_tail[:, g:g + 1])) for g, (k_g, v_g) in enumerate(mine)]

    key_lane = iota((1, keys_all), 1)
    key_block = (
        ((z - key_lane // tokens) * n_inner + x) * per_piece + lax.rem(key_lane, tokens) // BLK
    )
    key_pos = key_block * BLK + lax.rem(key_lane, BLK)
    listed = list_ref[...]
    for b in range(per_piece):
        member = key_block == listed[b:b + 1, 0:1]
        for i in range(1, listed.shape[1]):
            member = jnp.logical_or(member, key_block == listed[b:b + 1, i:i + 1])
        limit = jnp.where(member, key_pos, jnp.int32(2**30))
        first = (z * n_inner + x) * tokens + b * BLK
        query = first + iota((BLK * rep, 1), 0) // rep
        bias[b * BLK * rep:(b + 1) * BLK * rep, :] = jnp.where(limit <= query, 0.0, -1e30)

    for o in range(1, n_inner):
        x_copy(o).wait_recv()

    @pl.when(has_next)
    def _():
        l_hop(0).start()

    q_copy.wait()
    qf = qbuf[...].astype(F32)
    for g in range(kv):
        qs[g] = qf[:, g * rep:(g + 1) * rep, :].reshape(rows, width).astype(BF16)

    def within(g):
        k_g, v_g = mine[g][0], mine[g][1].astype(BF16)
        diff = cum_row[:, g:g + 1] - cum_lane[g:g + 1, :]
        weight = jnp.where(seen, jnp.exp(jnp.minimum(diff, 0.0)), 0.0)
        hi, lo = halves(dot(qs[g], k_g, ((1,), (1,))) * weight)
        lin[g] = dot(
            jnp.concatenate([hi, lo], axis=1), jnp.concatenate([v_g, v_g], axis=0))

    state = [jnp.zeros((width, width), F32) for _ in range(kv)]
    gap = [jnp.zeros((1, 1), F32) for _ in range(kv)]

    def totals(j):
        t = jnp.sum(ldbuf[j].reshape(n_inner * LD_ROWS, tokens), axis=1, keepdims=True)
        return [[t[o * LD_ROWS + g:o * LD_ROWS + g + 1, :] for o in range(n_inner)]
                for g in range(kv)]

    for j in range(1, n_seq):

        @pl.when(z < j)
        def _():
            kbuf[j] = jnp.zeros_like(kbuf[j])
            vbuf[j] = jnp.zeros_like(vbuf[j])

        relay(k_hop, j)
        if j == 1:
            within(0)
        relay(v_hop, j)
        relay(l_hop, j)
        if j == 1:
            for g in range(1, kv):
                within(g)
        row = totals(j)
        tail = dot(after, ldbuf[j, 0], ((1,), (1,)), HIGH)
        for g, (k_g, v_g) in enumerate(split(j)):
            rest = gap[g]
            for o in range(1, n_inner):
                rest = rest + jnp.where(x + o < n_inner, row[g][o], 0.0)
            state[g] = state[g] + outer(k_g, v_g * jnp.exp(tail[:, g:g + 1] + rest))
            gap[g] = gap[g] + sum(row[g])

    row = totals(0)
    before = []
    for g in range(kv):
        past = jnp.zeros((1, 1), F32)
        for o in range(1, n_inner):
            past = past + jnp.where(x + o >= n_inner, row[g][o], 0.0)
        before.append(past)
        msg[0, g] = state[g]
        msg[1, g] = state[g] * jnp.exp(past + row[g][0]) + own[g]

    def m_copy(o):
        to = lax.rem(x + o, n_inner)
        return pltpu.make_async_remote_copy(
            src_ref=msg.at[jnp.where(to > x, 1, 0)], dst_ref=got.at[o],
            send_sem=m_send.at[o], recv_sem=m_recv.at[o],
            device_id={"inner": to}, device_id_type=MESH)

    for o in range(1, n_inner):
        m_copy(o).start()

    step = min(rows, 256)
    scale = width ** (-0.5) * LOG2E

    @pl.loop(0, rows // step)
    def _(c):
        at = pl.ds(pl.multiple_of(c * step, step), step)
        for g in range(kv):
            score = dot(qs[g, at, :], kd[g], ((1,), (1,))) + bias[at, :]
            top = jnp.max(score, axis=1, keepdims=True)
            expo = jnp.exp2((score - top) * scale)
            denom = jnp.sum(expo, axis=1, keepdims=True)
            sp[g, at, :] = dot(expo.astype(BF16), vd[g]) / denom

    prior = [state[g] * jnp.exp(before[g]) for g in range(kv)]
    for o in range(1, n_inner):
        m_copy(o).wait_recv()
        for g in range(kv):
            later = jnp.zeros((1, 1), F32)
            for r in range(n_inner - o + 1, n_inner):
                later = later + row[g][r]
            prior[g] = prior[g] + got[o, g] * jnp.exp(jnp.where(x >= o, later, before[g]))

    done = []
    for g in range(kv):
        hi, lo = halves(prior[g])
        q_g = qs[g]
        inter = dot(
            jnp.concatenate([q_g, q_g], axis=1), jnp.concatenate([hi, lo], axis=0))
        linear = lin[g] + inter * jnp.exp(cum_row[:, g:g + 1])
        norm = lax.rsqrt(jnp.mean(linear * linear, axis=1, keepdims=True) + 1e-6)
        scaled = (linear * norm).reshape(tokens, rep, width) * gain_ref[g * rep:(g + 1) * rep, :][None]
        done.append(scaled + sp[g].reshape(tokens, rep, width))
    out_ref[...] = jnp.concatenate(done, axis=1).astype(out_ref.dtype)

    for j in range(n_seq - 1):

        @pl.when((z >= j) & has_next)
        def _():
            for hops in (k_hop, v_hop, l_hop):
                hops(j).wait_send()

    for o in range(1, n_inner):
        x_copy(o).wait_send()
        m_copy(o).wait_send()


def shards(n_seq, n_inner, queries, keys, values, log_decay, gain, block_list):
    tokens, heads, width = queries.shape
    kv = keys.shape[1]
    rows = tokens * (heads // kv)
    vmem = pl.BlockSpec(memory_space=pltpu.VMEM)
    anywhere = pl.BlockSpec(memory_space=pl.ANY)
    dma = pltpu.SemaphoreType.DMA
    return pl.pallas_call(
        functools.partial(kernel, n_seq, n_inner, kv),
        out_shape=jax.ShapeDtypeStruct(queries.shape, queries.dtype),
        in_specs=[anywhere, anywhere, anywhere, anywhere, vmem, vmem],
        out_specs=vmem,
        scratch_shapes=[
            pltpu.VMEM(queries.shape, BF16),
            pltpu.VMEM((n_seq, kv * tokens, width), BF16),
            pltpu.VMEM((n_seq, kv * tokens, width), BF16),
            pltpu.VMEM((n_seq, n_inner, LD_ROWS, tokens), F32),
            pltpu.VMEM((kv, rows, width), BF16),
            pltpu.VMEM((kv, n_seq * tokens, width), BF16),
            pltpu.VMEM((kv, n_seq * tokens, width), BF16),
            pltpu.VMEM((rows, n_seq * tokens), F32),
            pltpu.VMEM((kv, rows, width), F32),
            pltpu.VMEM((kv, rows, width), F32),
            pltpu.VMEM((2, kv, width, width), F32),
            pltpu.VMEM((n_inner, kv, width, width), F32),
            dma((4,)),
            dma((n_seq,)), dma((n_seq,)), dma((n_seq,)), dma((n_seq,)),
            dma((n_seq,)), dma((n_seq,)), dma((n_inner,)), dma((n_inner,)),
            dma((n_inner,)), dma((n_inner,)),
        ],
        compiler_params=pltpu.CompilerParams(collective_id=0, has_side_effects=True),
        name="prefill",
    )(
        queries, keys.reshape(tokens * kv, width), values.reshape(tokens * kv, width),
        log_decay.T, gain, block_list,
    )


def solution(mesh):
    return jax.shard_map(
        functools.partial(shards, mesh.shape["seq"], mesh.shape["inner"]),
        mesh=mesh,
        in_specs=(
            P(("groups", "seq", "inner"), "head", None),
            P(("groups", "seq", "inner"), "head", None),
            P(("groups", "seq", "inner"), "head", None),
            P(("groups", "seq", "inner"), "head"),
            P("head", None),
            P(("groups", "seq", "inner"), None),
        ),
        out_specs=P(("groups", "seq", "inner"), "head", None),
        check_vma=False,
    )
```

```python
import functools

import jax
import jax.numpy as jnp
from jax import lax
from jax.experimental import pallas as pl
from jax.experimental.pallas import tpu as pltpu
from jax.sharding import PartitionSpec as P

BLK = 64
HIGH = lax.Precision.HIGHEST
MESH = pl.DeviceIdType.MESH
LD_ROWS = 8
F32 = jnp.float32
BF16 = jnp.bfloat16
LOG2E = 1.4426950408889634


def iota(shape, dim):
    return lax.broadcasted_iota(jnp.int32, shape, dim)


def dot(a, b, dims=((1,), (0,)), precision=None):
    return lax.dot_general(
        a, b, (dims, ((), ())), precision=precision, preferred_element_type=F32
    )


def halves(x):
    hi = x.astype(BF16)
    return hi, (x - hi.astype(F32)).astype(BF16)


def kernel(
    n_seq, n_inner, kv,
    q_hbm, k_hbm, v_hbm, ld_hbm, gain_ref, list_ref,
    out_ref,
    qbuf, kbuf, vbuf, ldbuf, qs, kd, vd, bias, lin, sp, msg, got, own_msg, own_got,
    local_sem, k_send, k_recv, v_send, v_recv, l_send, l_recv, x_send, x_recv,
    m_send, m_recv, o_send, o_recv,
):
    z = lax.axis_index("seq")
    x = lax.axis_index("inner")
    tokens, heads, width = qbuf.shape
    rep = heads // kv
    rows = tokens * rep
    per_piece = tokens // BLK
    keys_all = n_seq * tokens
    has_next, has_last = z < n_seq - 1, z > 0

    ldbuf[...] = jnp.zeros_like(ldbuf)
    q_copy = pltpu.make_async_copy(q_hbm, qbuf, local_sem.at[0])
    k_copy = pltpu.make_async_copy(k_hbm, kbuf.at[0], local_sem.at[1])
    v_copy = pltpu.make_async_copy(v_hbm, vbuf.at[0], local_sem.at[2])
    l_copy = pltpu.make_async_copy(ld_hbm, ldbuf.at[0, 0, 0:kv], local_sem.at[3])
    for copy in (l_copy, k_copy, v_copy, q_copy):
        copy.start()

    barrier = pltpu.get_barrier_semaphore()

    @pl.when(has_next)
    def _():
        pl.semaphore_signal(barrier, inc=1, device_id={"seq": z + 1}, device_id_type=MESH)

    @pl.when(has_last)
    def _():
        pl.semaphore_signal(barrier, inc=1, device_id={"seq": z - 1}, device_id_type=MESH)

    for o in range(1, n_inner):
        pl.semaphore_signal(
            barrier, inc=1, device_id={"inner": lax.rem(x + o, n_inner)}, device_id_type=MESH)
    ends = jnp.where(has_next, 1, 0) + jnp.where(has_last, 1, 0)
    pl.semaphore_wait(barrier, n_inner - 1 + ends)

    def hop(src, dst, send, recv):
        return pltpu.make_async_remote_copy(
            src_ref=src, dst_ref=dst, send_sem=send, recv_sem=recv,
            device_id={"seq": z + 1}, device_id_type=MESH)

    def k_hop(j):
        return hop(
            k_hbm if j == 0 else kbuf.at[j], kbuf.at[j + 1], k_send.at[j], k_recv.at[j + 1])

    def v_hop(j):
        return hop(
            v_hbm if j == 0 else vbuf.at[j], vbuf.at[j + 1], v_send.at[j], v_recv.at[j + 1])

    def l_hop(j):
        return hop(
            ldbuf.at[j, :, 0:kv], ldbuf.at[j + 1, :, 0:kv], l_send.at[j], l_recv.at[j + 1])

    def relay(hops, j):
        @pl.when(z >= j)
        def _():
            hops(j - 1).wait_recv()

        if j < n_seq - 1:

            @pl.when((z >= j) & has_next)
            def _():
                hops(j).start()

    def x_copy(o):
        return pltpu.make_async_remote_copy(
            src_ref=ld_hbm, dst_ref=ldbuf.at[0, n_inner - o, 0:kv], send_sem=x_send.at[o],
            recv_sem=x_recv.at[o], device_id={"inner": lax.rem(x + o, n_inner)},
            device_id_type=MESH)

    @pl.when(has_next)
    def _():
        k_hop(0).start()
        v_hop(0).start()

    for o in range(1, n_inner):
        x_copy(o).start()

    lanes = iota((kv * tokens, kv * tokens), 1)
    subs = iota((kv * tokens, kv * tokens), 0)
    by_head = jnp.where(
        lanes == lax.rem(subs, tokens) * kv + subs // tokens, 1.0, 0.0
    ).astype(BF16)

    l_copy.wait()
    ld = ldbuf[0, 0]
    upto = jnp.where(iota((tokens, tokens), 0) <= iota((tokens, tokens), 1), 1.0, 0.0)
    after = jnp.where(iota((tokens, tokens), 0) < iota((tokens, tokens), 1), 1.0, 0.0)
    cum_lane = dot(ld, upto, precision=HIGH)
    row_tok = iota((rows, tokens), 0) // rep
    lane_tok = iota((rows, tokens), 1)
    seen = row_tok >= lane_tok
    cum_row = dot(jnp.where(seen, 1.0, 0.0), ld, ((1,), (1,)), HIGH)
    own_tail = dot(after, ld, ((1,), (1,)), HIGH)

    def outer(k, weighted):
        hi, lo = halves(weighted)
        return dot(
            jnp.concatenate([k, k], axis=0), jnp.concatenate([hi, lo], axis=0), ((0,), (0,)))

    def split(j):
        k_j = dot(by_head, kbuf[j]).astype(BF16)
        v_j = dot(by_head, vbuf[j])
        out = []
        for g in range(kv):
            k_g = k_j[g * tokens:(g + 1) * tokens]
            v_g = v_j[g * tokens:(g + 1) * tokens]
            kd[g, j * tokens:(j + 1) * tokens, :] = k_g
            vd[g, j * tokens:(j + 1) * tokens, :] = v_g.astype(BF16)
            out.append((k_g, v_g))
        return out

    k_copy.wait()
    v_copy.wait()
    mine = split(0)
    own = [outer(k_g, v_g * jnp.exp(own_tail[:, g:g + 1])) for g, (k_g, v_g) in enumerate(mine)]
    for g in range(kv):
        own_msg[g] = own[g]

    def o_copy(o):
        return pltpu.make_async_remote_copy(
            src_ref=own_msg, dst_ref=own_got.at[o], send_sem=o_send.at[o],
            recv_sem=o_recv.at[o], device_id={"inner": lax.rem(x + o, n_inner)},
            device_id_type=MESH)

    for o in range(1, n_inner):
        x_copy(o).wait_recv()

    @pl.when(has_next)
    def _():
        l_hop(0).start()

    for o in range(1, n_inner):
        o_copy(o).start()

    def visibility():
        key_lane = iota((1, keys_all), 1)
        key_block = (
            ((z - key_lane // tokens) * n_inner + x) * per_piece + lax.rem(key_lane, tokens) // BLK
        )
        key_pos = key_block * BLK + lax.rem(key_lane, BLK)
        listed = list_ref[...]
        for b in range(per_piece):
            member = key_block == listed[b:b + 1, 0:1]
            for i in range(1, listed.shape[1]):
                member = jnp.logical_or(member, key_block == listed[b:b + 1, i:i + 1])
            limit = jnp.where(member, key_pos, jnp.int32(2**30))
            first = (z * n_inner + x) * tokens + b * BLK
            query = first + iota((BLK * rep, 1), 0) // rep
            bias[b * BLK * rep:(b + 1) * BLK * rep, :] = jnp.where(limit <= query, 0.0, -1e30)

    def take_queries():
        q_copy.wait()
        qf = qbuf[...].astype(F32)
        for g in range(kv):
            qs[g] = qf[:, g * rep:(g + 1) * rep, :].reshape(rows, width).astype(BF16)

    def within(g):
        k_g, v_g = mine[g][0], mine[g][1].astype(BF16)
        diff = cum_row[:, g:g + 1] - cum_lane[g:g + 1, :]
        weight = jnp.where(seen, jnp.exp(jnp.minimum(diff, 0.0)), 0.0)
        hi, lo = halves(dot(qs[g], k_g, ((1,), (1,))) * weight)
        lin[g] = dot(
            jnp.concatenate([hi, lo], axis=1), jnp.concatenate([v_g, v_g], axis=0))

    state = [jnp.zeros((width, width), F32) for _ in range(kv)]
    gap = [jnp.zeros((1, 1), F32) for _ in range(kv)]

    def totals(j):
        t = jnp.sum(ldbuf[j].reshape(n_inner * LD_ROWS, tokens), axis=1, keepdims=True)
        return [[t[o * LD_ROWS + g:o * LD_ROWS + g + 1, :] for o in range(n_inner)]
                for g in range(kv)]

    def absorb(j):
        row = totals(j)
        tail = dot(after, ldbuf[j, 0], ((1,), (1,)), HIGH)
        for g, (k_g, v_g) in enumerate(split(j)):
            rest = gap[g]
            for o in range(1, n_inner):
                rest = rest + jnp.where(x + o < n_inner, row[g][o], 0.0)
            state[g] = state[g] + outer(k_g, v_g * jnp.exp(tail[:, g:g + 1] + rest))
            gap[g] = gap[g] + sum(row[g])

    def first_head():
        take_queries()
        within(0)

    work = [visibility, first_head] + [functools.partial(within, g) for g in range(1, kv)]
    for j in range(1, n_seq):

        @pl.when(z < j)
        def _():
            kbuf[j] = jnp.zeros_like(kbuf[j])
            vbuf[j] = jnp.zeros_like(vbuf[j])

        relay(k_hop, j)
        if work:
            work.pop(0)()
        relay(v_hop, j)
        relay(l_hop, j)
        work.append(functools.partial(absorb, j))
        work.pop(0)()
    for item in work:
        item()

    row = totals(0)
    before = []
    for g in range(kv):
        past, ahead = jnp.zeros((1, 1), F32), jnp.zeros((1, 1), F32)
        for o in range(1, n_inner):
            past = past + jnp.where(x + o >= n_inner, row[g][o], 0.0)
            ahead = ahead + jnp.where(x + o < n_inner, row[g][o], 0.0)
        before.append(past)
        msg[g] = state[g] * jnp.exp(sum(row[g])) + own[g] * jnp.exp(ahead)

    def m_copy(o):
        return pltpu.make_async_remote_copy(
            src_ref=msg, dst_ref=got.at[o], send_sem=m_send.at[o], recv_sem=m_recv.at[o],
            device_id={"seq": z + 1, "inner": lax.rem(x + o, n_inner)}, device_id_type=MESH)

    @pl.when(has_next)
    def _():
        for o in range(1, n_inner):
            m_copy(o).start()

    step = min(rows, 256)
    scale = width ** (-0.5) * LOG2E

    @pl.loop(0, rows // step, unroll=True)
    def _(c):
        at = pl.ds(pl.multiple_of(c * step, step), step)
        for g in range(kv):
            score = dot(qs[g, at, :], kd[g], ((1,), (1,))) + bias[at, :]
            top = jnp.max(score, axis=1, keepdims=True)
            expo = jnp.exp2((score - top) * scale)
            denom = jnp.sum(expo, axis=1, keepdims=True)
            sp[g, at, :] = dot(expo.astype(BF16), vd[g]) / denom


    @pl.when(has_last)
    def _():
        for o in range(1, n_inner):
            m_copy(o).wait_recv()

    @pl.when(z == 0)
    def _():
        got[...] = jnp.zeros_like(got)

    prior = []
    for g in range(kv):
        at_row = state[g]
        for o in range(1, n_inner):
            at_row = at_row + got[o, g]
        prior.append(at_row * jnp.exp(before[g]))
    for o in range(1, n_inner):
        o_copy(o).wait_recv()
        for g in range(kv):
            later = jnp.zeros((1, 1), F32)
            for r in range(n_inner - o + 1, n_inner):
                later = later + row[g][r]
            prior[g] = prior[g] + own_got[o, g] * jnp.where(x >= o, jnp.exp(later), 0.0)

    done = []
    for g in range(kv):
        hi, lo = halves(prior[g])
        q_g = qs[g]
        inter = dot(
            jnp.concatenate([q_g, q_g], axis=1), jnp.concatenate([hi, lo], axis=0))
        linear = lin[g] + inter * jnp.exp(cum_row[:, g:g + 1])
        norm = lax.rsqrt(jnp.mean(linear * linear, axis=1, keepdims=True) + 1e-6)
        scaled = (linear * norm).reshape(tokens, rep, width) * gain_ref[g * rep:(g + 1) * rep, :][None]
        done.append(scaled + sp[g].reshape(tokens, rep, width))
    out_ref[...] = jnp.concatenate(done, axis=1).astype(out_ref.dtype)

    for j in range(n_seq - 1):

        @pl.when((z >= j) & has_next)
        def _():
            for hops in (k_hop, v_hop, l_hop):
                hops(j).wait_send()

    for o in range(1, n_inner):
        x_copy(o).wait_send()
        o_copy(o).wait_send()

    @pl.when(has_next)
    def _():
        for o in range(1, n_inner):
            m_copy(o).wait_send()


def shards(n_seq, n_inner, queries, keys, values, log_decay, gain, block_list):
    tokens, heads, width = queries.shape
    kv = keys.shape[1]
    rows = tokens * (heads // kv)
    vmem = pl.BlockSpec(memory_space=pltpu.VMEM)
    anywhere = pl.BlockSpec(memory_space=pl.ANY)
    dma = pltpu.SemaphoreType.DMA
    return pl.pallas_call(
        functools.partial(kernel, n_seq, n_inner, kv),
        out_shape=jax.ShapeDtypeStruct(queries.shape, queries.dtype),
        in_specs=[anywhere, anywhere, anywhere, anywhere, vmem, vmem],
        out_specs=vmem,
        scratch_shapes=[
            pltpu.VMEM(queries.shape, BF16),
            pltpu.VMEM((n_seq, kv * tokens, width), BF16),
            pltpu.VMEM((n_seq, kv * tokens, width), BF16),
            pltpu.VMEM((n_seq, n_inner, LD_ROWS, tokens), F32),
            pltpu.VMEM((kv, rows, width), BF16),
            pltpu.VMEM((kv, n_seq * tokens, width), BF16),
            pltpu.VMEM((kv, n_seq * tokens, width), BF16),
            pltpu.VMEM((rows, n_seq * tokens), F32),
            pltpu.VMEM((kv, rows, width), F32),
            pltpu.VMEM((kv, rows, width), F32),
            pltpu.VMEM((kv, width, width), F32),
            pltpu.VMEM((n_inner, kv, width, width), F32),
            pltpu.VMEM((kv, width, width), F32),
            pltpu.VMEM((n_inner, kv, width, width), F32),
            dma((4,)),
            dma((n_seq,)), dma((n_seq,)), dma((n_seq,)), dma((n_seq,)),
            dma((n_seq,)), dma((n_seq,)), dma((n_inner,)), dma((n_inner,)),
            dma((n_inner,)), dma((n_inner,)), dma((n_inner,)), dma((n_inner,)),
        ],
        compiler_params=pltpu.CompilerParams(collective_id=0, has_side_effects=True),
        name="prefill",
    )(
        queries, keys.reshape(tokens * kv, width), values.reshape(tokens * kv, width),
        log_decay.T, gain, block_list,
    )


def solution(mesh):
    return jax.shard_map(
        functools.partial(shards, mesh.shape["seq"], mesh.shape["inner"]),
        mesh=mesh,
        in_specs=(
            P(("groups", "seq", "inner"), "head", None),
            P(("groups", "seq", "inner"), "head", None),
            P(("groups", "seq", "inner"), "head", None),
            P(("groups", "seq", "inner"), "head"),
            P("head", None),
            P(("groups", "seq", "inner"), None),
        ),
        out_specs=P(("groups", "seq", "inner"), "head", None),
        check_vma=False,
    )
```

```python
import functools

import jax
import jax.numpy as jnp
from jax import lax
from jax.experimental import pallas as pl
from jax.experimental.pallas import tpu as pltpu
from jax.sharding import PartitionSpec as P

BLK = 64
HIGH = lax.Precision.HIGHEST
MESH = pl.DeviceIdType.MESH
LD_ROWS = 8
F32 = jnp.float32
BF16 = jnp.bfloat16
LOG2E = 1.4426950408889634


def iota(shape, dim):
    return lax.broadcasted_iota(jnp.int32, shape, dim)


def dot(a, b, dims=((1,), (0,)), precision=None):
    return lax.dot_general(
        a, b, (dims, ((), ())), precision=precision, preferred_element_type=F32
    )


def halves(x):
    hi = x.astype(BF16)
    return hi, (x - hi.astype(F32)).astype(BF16)


def kernel(
    n_seq, n_inner, kv,
    q_hbm, k_hbm, v_hbm, ld_hbm, gain_ref, list_ref,
    out_ref,
    qbuf, kbuf, vbuf, ldbuf, qs, kd, vd, bias, lin, sp, msg, got, own_msg, own_got,
    local_sem, k_send, k_recv, v_send, v_recv, l_send, l_recv, x_send, x_recv,
    m_send, m_recv, o_send, o_recv,
):
    z = lax.axis_index("seq")
    x = lax.axis_index("inner")
    tokens, heads, width = qbuf.shape
    rep = heads // kv
    rows = tokens * rep
    per_piece = tokens // BLK
    keys_all = n_seq * tokens
    has_next, has_last = z < n_seq - 1, z > 0

    ldbuf[...] = jnp.zeros_like(ldbuf)
    q_copy = pltpu.make_async_copy(q_hbm, qbuf, local_sem.at[0])
    k_copy = pltpu.make_async_copy(k_hbm, kbuf.at[0], local_sem.at[1])
    v_copy = pltpu.make_async_copy(v_hbm, vbuf.at[0], local_sem.at[2])
    l_copy = pltpu.make_async_copy(ld_hbm, ldbuf.at[0, 0, 0:kv], local_sem.at[3])
    for copy in (l_copy, k_copy, v_copy, q_copy):
        copy.start()

    barrier = pltpu.get_barrier_semaphore()

    @pl.when(has_next)
    def _():
        pl.semaphore_signal(barrier, inc=1, device_id={"seq": z + 1}, device_id_type=MESH)

    @pl.when(has_last)
    def _():
        pl.semaphore_signal(barrier, inc=1, device_id={"seq": z - 1}, device_id_type=MESH)

    for o in range(1, n_inner):
        pl.semaphore_signal(
            barrier, inc=1, device_id={"inner": lax.rem(x + o, n_inner)}, device_id_type=MESH)
    ends = jnp.where(has_next, 1, 0) + jnp.where(has_last, 1, 0)
    pl.semaphore_wait(barrier, n_inner - 1 + ends)

    def hop(src, dst, send, recv):
        return pltpu.make_async_remote_copy(
            src_ref=src, dst_ref=dst, send_sem=send, recv_sem=recv,
            device_id={"seq": z + 1}, device_id_type=MESH)

    def k_hop(j):
        return hop(
            k_hbm if j == 0 else kbuf.at[j], kbuf.at[j + 1], k_send.at[j], k_recv.at[j + 1])

    def v_hop(j):
        return hop(
            v_hbm if j == 0 else vbuf.at[j], vbuf.at[j + 1], v_send.at[j], v_recv.at[j + 1])

    def l_hop(j):
        return hop(
            ldbuf.at[j, :, 0:kv], ldbuf.at[j + 1, :, 0:kv], l_send.at[j], l_recv.at[j + 1])

    def relay(hops, j):
        @pl.when(z >= j)
        def _():
            hops(j - 1).wait_recv()

        if j < n_seq - 1:

            @pl.when((z >= j) & has_next)
            def _():
                hops(j).start()

    def x_copy(o):
        return pltpu.make_async_remote_copy(
            src_ref=ld_hbm, dst_ref=ldbuf.at[0, n_inner - o, 0:kv], send_sem=x_send.at[o],
            recv_sem=x_recv.at[o], device_id={"inner": lax.rem(x + o, n_inner)},
            device_id_type=MESH)

    @pl.when(has_next)
    def _():
        k_hop(0).start()
        v_hop(0).start()

    for o in range(1, n_inner):
        x_copy(o).start()

    lanes = iota((kv * tokens, kv * tokens), 1)
    subs = iota((kv * tokens, kv * tokens), 0)
    by_head = jnp.where(
        lanes == lax.rem(subs, tokens) * kv + subs // tokens, 1.0, 0.0
    ).astype(BF16)

    l_copy.wait()
    ld = ldbuf[0, 0]
    upto = jnp.where(iota((tokens, tokens), 0) <= iota((tokens, tokens), 1), 1.0, 0.0)
    after = jnp.where(iota((tokens, tokens), 0) < iota((tokens, tokens), 1), 1.0, 0.0)
    cum_lane = dot(ld, upto, precision=HIGH)
    row_tok = iota((rows, tokens), 0) // rep
    lane_tok = iota((rows, tokens), 1)
    seen = row_tok >= lane_tok
    cum_row = dot(jnp.where(seen, 1.0, 0.0), ld, ((1,), (1,)), HIGH)
    own_tail = dot(after, ld, ((1,), (1,)), HIGH)

    def outer(k, weighted):
        hi, lo = halves(weighted)
        return dot(
            jnp.concatenate([k, k], axis=0), jnp.concatenate([hi, lo], axis=0), ((0,), (0,)))

    def split(j):
        k_j = dot(by_head, kbuf[j]).astype(BF16)
        v_j = dot(by_head, vbuf[j])
        out = []
        for g in range(kv):
            k_g = k_j[g * tokens:(g + 1) * tokens]
            v_g = v_j[g * tokens:(g + 1) * tokens]
            kd[g, j * tokens:(j + 1) * tokens, :] = k_g
            vd[g, j * tokens:(j + 1) * tokens, :] = v_g.astype(BF16)
            out.append((k_g, v_g))
        return out

    k_copy.wait()
    v_copy.wait()
    mine = split(0)
    own = [outer(k_g, v_g * jnp.exp(own_tail[:, g:g + 1])) for g, (k_g, v_g) in enumerate(mine)]
    for g in range(kv):
        own_msg[g] = own[g]

    def o_copy(o):
        return pltpu.make_async_remote_copy(
            src_ref=own_msg, dst_ref=own_got.at[o], send_sem=o_send.at[o],
            recv_sem=o_recv.at[o], device_id={"inner": lax.rem(x + o, n_inner)},
            device_id_type=MESH)

    for o in range(1, n_inner):
        x_copy(o).wait_recv()

    @pl.when(has_next)
    def _():
        l_hop(0).start()

    for o in range(1, n_inner):
        o_copy(o).start()

    def visibility():
        key_lane = iota((1, keys_all), 1)
        key_block = (
            ((z - key_lane // tokens) * n_inner + x) * per_piece + lax.rem(key_lane, tokens) // BLK
        )
        key_pos = key_block * BLK + lax.rem(key_lane, BLK)
        listed = list_ref[...]
        for b in range(per_piece):
            member = key_block == listed[b:b + 1, 0:1]
            for i in range(1, listed.shape[1]):
                member = jnp.logical_or(member, key_block == listed[b:b + 1, i:i + 1])
            limit = jnp.where(member, key_pos, jnp.int32(2**30))
            first = (z * n_inner + x) * tokens + b * BLK
            query = first + iota((BLK * rep, 1), 0) // rep
            bias[b * BLK * rep:(b + 1) * BLK * rep, :] = jnp.where(limit <= query, 0.0, -1e30)

    def take_queries():
        q_copy.wait()
        qf = qbuf[...].astype(F32)
        for g in range(kv):
            qs[g] = qf[:, g * rep:(g + 1) * rep, :].reshape(rows, width).astype(BF16)

    def within(g):
        k_g, v_g = mine[g][0], mine[g][1].astype(BF16)
        diff = cum_row[:, g:g + 1] - cum_lane[g:g + 1, :]
        weight = jnp.where(seen, jnp.exp(jnp.minimum(diff, 0.0)), 0.0)
        hi, lo = halves(dot(qs[g], k_g, ((1,), (1,))) * weight)
        lin[g] = dot(
            jnp.concatenate([hi, lo], axis=1), jnp.concatenate([v_g, v_g], axis=0))

    state = [jnp.zeros((width, width), F32) for _ in range(kv)]
    gap = [jnp.zeros((1, 1), F32) for _ in range(kv)]

    def totals(j):
        t = jnp.sum(ldbuf[j].reshape(n_inner * LD_ROWS, tokens), axis=1, keepdims=True)
        return [[t[o * LD_ROWS + g:o * LD_ROWS + g + 1, :] for o in range(n_inner)]
                for g in range(kv)]

    def absorb(j):
        row = totals(j)
        tail = dot(after, ldbuf[j, 0], ((1,), (1,)), HIGH)
        for g, (k_g, v_g) in enumerate(split(j)):
            rest = gap[g]
            for o in range(1, n_inner):
                rest = rest + jnp.where(x + o < n_inner, row[g][o], 0.0)
            state[g] = state[g] + outer(k_g, v_g * jnp.exp(tail[:, g:g + 1] + rest))
            gap[g] = gap[g] + sum(row[g])

    def first_head():
        take_queries()
        within(0)

    work = [visibility, first_head] + [functools.partial(within, g) for g in range(1, kv)]
    for j in range(1, n_seq):

        @pl.when(z < j)
        def _():
            kbuf[j] = jnp.zeros_like(kbuf[j])
            vbuf[j] = jnp.zeros_like(vbuf[j])

        relay(k_hop, j)
        if work:
            work.pop(0)()
        relay(v_hop, j)
        relay(l_hop, j)
        work.append(functools.partial(absorb, j))
        work.pop(0)()
    for item in work:
        item()

    row = totals(0)
    before = []
    for g in range(kv):
        past, ahead = jnp.zeros((1, 1), F32), jnp.zeros((1, 1), F32)
        for o in range(1, n_inner):
            past = past + jnp.where(x + o >= n_inner, row[g][o], 0.0)
            ahead = ahead + jnp.where(x + o < n_inner, row[g][o], 0.0)
        before.append(past)
        msg[g] = state[g] * jnp.exp(sum(row[g])) + own[g] * jnp.exp(ahead)

    def m_copy(o):
        return pltpu.make_async_remote_copy(
            src_ref=msg, dst_ref=got.at[o], send_sem=m_send.at[o], recv_sem=m_recv.at[o],
            device_id={"seq": z + 1, "inner": lax.rem(x + o, n_inner)}, device_id_type=MESH)

    @pl.when(has_next)
    def _():
        for o in range(1, n_inner):
            m_copy(o).start()

    step = min(rows, 512)
    scale = width ** (-0.5) * LOG2E

    @pl.loop(0, rows // step, unroll=True)
    def _(c):
        at = pl.ds(pl.multiple_of(c * step, step), step)
        for g in range(kv):
            score = dot(qs[g, at, :], kd[g], ((1,), (1,))) + bias[at, :]
            top = jnp.max(score, axis=1, keepdims=True)
            expo = jnp.exp2((score - top) * scale)
            denom = jnp.sum(expo, axis=1, keepdims=True)
            sp[g, at, :] = dot(expo.astype(BF16), vd[g]) / denom


    @pl.when(has_last)
    def _():
        for o in range(1, n_inner):
            m_copy(o).wait_recv()

    @pl.when(z == 0)
    def _():
        got[...] = jnp.zeros_like(got)

    prior = []
    for g in range(kv):
        at_row = state[g]
        for o in range(1, n_inner):
            at_row = at_row + got[o, g]
        prior.append(at_row * jnp.exp(before[g]))
    for o in range(1, n_inner):
        o_copy(o).wait_recv()
        for g in range(kv):
            later = jnp.zeros((1, 1), F32)
            for r in range(n_inner - o + 1, n_inner):
                later = later + row[g][r]
            prior[g] = prior[g] + own_got[o, g] * jnp.where(x >= o, jnp.exp(later), 0.0)

    done = []
    for g in range(kv):
        hi, lo = halves(prior[g])
        q_g = qs[g]
        inter = dot(
            jnp.concatenate([q_g, q_g], axis=1), jnp.concatenate([hi, lo], axis=0))
        linear = lin[g] + inter * jnp.exp(cum_row[:, g:g + 1])
        norm = lax.rsqrt(jnp.mean(linear * linear, axis=1, keepdims=True) + 1e-6)
        scaled = (linear * norm).reshape(tokens, rep, width) * gain_ref[g * rep:(g + 1) * rep, :][None]
        done.append(scaled + sp[g].reshape(tokens, rep, width))
    out_ref[...] = jnp.concatenate(done, axis=1).astype(out_ref.dtype)

    for j in range(n_seq - 1):

        @pl.when((z >= j) & has_next)
        def _():
            for hops in (k_hop, v_hop, l_hop):
                hops(j).wait_send()

    for o in range(1, n_inner):
        x_copy(o).wait_send()
        o_copy(o).wait_send()

    @pl.when(has_next)
    def _():
        for o in range(1, n_inner):
            m_copy(o).wait_send()


def shards(n_seq, n_inner, queries, keys, values, log_decay, gain, block_list):
    tokens, heads, width = queries.shape
    kv = keys.shape[1]
    rows = tokens * (heads // kv)
    vmem = pl.BlockSpec(memory_space=pltpu.VMEM)
    anywhere = pl.BlockSpec(memory_space=pl.ANY)
    dma = pltpu.SemaphoreType.DMA
    return pl.pallas_call(
        functools.partial(kernel, n_seq, n_inner, kv),
        out_shape=jax.ShapeDtypeStruct(queries.shape, queries.dtype),
        in_specs=[anywhere, anywhere, anywhere, anywhere, vmem, vmem],
        out_specs=vmem,
        scratch_shapes=[
            pltpu.VMEM(queries.shape, BF16),
            pltpu.VMEM((n_seq, kv * tokens, width), BF16),
            pltpu.VMEM((n_seq, kv * tokens, width), BF16),
            pltpu.VMEM((n_seq, n_inner, LD_ROWS, tokens), F32),
            pltpu.VMEM((kv, rows, width), BF16),
            pltpu.VMEM((kv, n_seq * tokens, width), BF16),
            pltpu.VMEM((kv, n_seq * tokens, width), BF16),
            pltpu.VMEM((rows, n_seq * tokens), F32),
            pltpu.VMEM((kv, rows, width), F32),
            pltpu.VMEM((kv, rows, width), F32),
            pltpu.VMEM((kv, width, width), F32),
            pltpu.VMEM((n_inner, kv, width, width), F32),
            pltpu.VMEM((kv, width, width), F32),
            pltpu.VMEM((n_inner, kv, width, width), F32),
            dma((4,)),
            dma((n_seq,)), dma((n_seq,)), dma((n_seq,)), dma((n_seq,)),
            dma((n_seq,)), dma((n_seq,)), dma((n_inner,)), dma((n_inner,)),
            dma((n_inner,)), dma((n_inner,)), dma((n_inner,)), dma((n_inner,)),
        ],
        compiler_params=pltpu.CompilerParams(collective_id=0, has_side_effects=True),
        name="prefill",
    )(
        queries, keys.reshape(tokens * kv, width), values.reshape(tokens * kv, width),
        log_decay.T, gain, block_list,
    )


def solution(mesh):
    return jax.shard_map(
        functools.partial(shards, mesh.shape["seq"], mesh.shape["inner"]),
        mesh=mesh,
        in_specs=(
            P(("groups", "seq", "inner"), "head", None),
            P(("groups", "seq", "inner"), "head", None),
            P(("groups", "seq", "inner"), "head", None),
            P(("groups", "seq", "inner"), "head"),
            P("head", None),
            P(("groups", "seq", "inner"), None),
        ),
        out_specs=P(("groups", "seq", "inner"), "head", None),
        check_vma=False,
    )
```
